32 devices in a mesh: rows: 16 (over z, y, x), cols: 2 (over core).
Axes of the slice: x: 2, y: 2, z: 4, core: 2. Of those that a mesh axis runs over, the one named last changes fastest.
Arguments:
- quantized: bfloat16 [3072, 384, 128], P('rows', 'cols'), may hold values from 0 to 127, as said below
- scales: bfloat16 [3072, 384], P('rows', 'cols'), may hold values from 0 to 1, as said below
- mode_one: float32 [3072, 32], P('rows'), may hold values from 0 to 40
- mode_two: bfloat16 [384, 32], P('cols'), may hold values from 0 to 1, as said below
- mode_three: bfloat16 [4096, 32], replicated, may hold values from 0 to 0.29882812
- core_tensor: float32 [32, 32, 32], P('rows'), may hold values from 0.0002 to 0.004
- slab_index: int32 [1], replicated, may hold values from 0 to 31
Outputs:
- new_one: float32 [3072, 32], P('rows')
- new_core: float32 [32, 32, 32], P('rows')
The draws below stay inside these ranges and needn't reach their ends.
Inputs may be any that keep to these rules, and one draw needn't show every extreme that they name: `quantized`: nonnegative integer values of an int8 quantization. `scales`: positive. `mode_two`: nonnegative.
All inputs are finite; a program needn't handle non-finite values.
Results may differ from the reference program's by a relative error of at most 0.0017.
Values sent between devices are 32-bit elements; how exact they have to be, the bound alone decides.
A program may use at most 64 MiB of HBM per device.

```python
import math
import jax
import jax.numpy as jnp
from jax import lax

ROWS_DEV = 192
DEPTH = 4096
SLAB = 128
RANK = 32
ALL_ROWS = 3072
ALL_COLS = 384


def draw_quantized(key, part):
    keys = jax.random.split(key, 5)
    row_level = jax.random.randint(keys[0], (ALL_ROWS,), 1, 5)
    col_level = jax.random.randint(keys[1], (ALL_COLS,), 1, 5)
    row_factor = jax.random.randint(keys[2], (ALL_ROWS, SLAB), 0, 4)
    col_factor = jax.random.randint(keys[3], (ALL_COLS, SLAB), 0, 4)
    noise = jax.random.randint(keys[4], (ALL_ROWS, ALL_COLS, SLAB), 0, 16)
    left = row_level[:, None] * row_factor
    right = col_level[:, None] * col_factor
    values = left[:, None, :] * right[None, :, :] + noise
    values = jnp.minimum(values, 127)
    return values.astype(jnp.float32).astype(jnp.bfloat16)


def draw_scales(key, part):
    positions = jnp.arange(ALL_ROWS, dtype=jnp.float32)
    rising = 1.0 + 2.0 * positions / max(ALL_ROWS - 1, 1)
    base = jnp.exp(jax.random.uniform(key, (ALL_ROWS, ALL_COLS), jnp.float32, 0.0, math.log(10.0)))
    return (base * rising[:, None] / 88.0).astype(jnp.bfloat16)


def draw_mode_two(key, part):
    uniform_part = jax.random.uniform(key, (ALL_COLS, RANK), jnp.float32, 0.0, 1.0)
    return (uniform_part * math.sqrt(3.0 / ALL_COLS)).astype(jnp.bfloat16)


def steps_of(key, extent, shards, least, high):
    level = 1.0
    for dim, blocks in shards:
        steps = jax.random.uniform(jax.random.fold_in(jax.random.fold_in(key, 6), dim), (blocks,), jnp.float32, least / len(shards), high / len(shards))
        level = level * jnp.repeat(jnp.exp(steps), extent[dim] // blocks).reshape((-1,) + (1,) * (len(extent) - 1 - dim))
    return level


def setup_inputs(seed: int = 0) -> dict:
    seeds = jax.random.split(jax.random.key(seed), 8)
    return {
        "quantized": draw_quantized(jax.random.fold_in(seeds[7], 71), 0),
        "scales": draw_scales(jax.random.fold_in(seeds[7], 71), 0),
        "mode_one": jnp.clip(40.0 * jax.random.uniform(seeds[2], (ALL_ROWS, RANK), jnp.float32) ** steps_of(seeds[2], (ALL_ROWS, RANK), ((0, 16),), -0.2, 0.2), 0.0, 40.0),
        "mode_two": draw_mode_two(jax.random.fold_in(seeds[7], 71), 0),
        "mode_three": jnp.clip(jax.random.uniform(seeds[4], (DEPTH, RANK), jnp.float32, 0.0, 0.29882812), 0.0, 0.29882812).astype(jnp.bfloat16),
        "core_tensor": jnp.clip(jnp.exp(math.log(0.004) - 2.9957323 * jax.random.uniform(seeds[5], (RANK, RANK, RANK), jnp.float32) ** steps_of(seeds[5], (RANK, RANK, RANK), ((0, 16),), -0.2, 0.2)), 0.0002, 0.004),
        "slab_index": jax.random.randint(seeds[6], (1,), 0, DEPTH // SLAB).astype(jnp.int32),
    }


def weight_gram(core_whole, gram_two, gram_three):
    highest = lax.Precision.HIGHEST
    left = jnp.einsum('rab,ac->rcb', core_whole, gram_two, precision=highest)
    left = jnp.einsum('rcb,bd->rcd', left, gram_three, precision=highest)
    flat = core_whole.reshape(core_whole.shape[0], -1)
    return jnp.dot(left.reshape(flat.shape), flat.T, precision=highest)

def hals_sweep(current, target, coupling):
    highest = lax.Precision.HIGHEST

    def column(position, values):
        where = jnp.asarray(position).astype(jnp.int32)
        weights = lax.dynamic_slice_in_dim(coupling, where, 1, 1)[:, 0]
        diagonal = lax.dynamic_index_in_dim(weights, where, 0, keepdims=False)
        wanted = lax.dynamic_slice_in_dim(target, where, 1, 1)[:, 0]
        before = lax.dynamic_slice_in_dim(values, where, 1, 1)[:, 0]
        fitted = jnp.dot(values, weights, precision=highest)
        after = jnp.maximum(before + (wanted - fitted) / diagonal, 0.0)
        return lax.dynamic_update_slice_in_dim(values, after[:, None], where, 1)
    return lax.fori_loop(0, coupling.shape[0], column, current)

def reference(quantized, scales, mode_one, mode_two, mode_three, core_tensor, slab_index):
    highest = lax.Precision.HIGHEST
    offset = (slab_index[0] * SLAB).astype(jnp.int32)
    chosen = lax.dynamic_slice_in_dim(mode_three, offset, SLAB, 0)
    two_wide = mode_two.astype(jnp.float32)
    chosen_wide = chosen.astype(jnp.float32)

    def project(block):
        block_values, block_scales = block
        tensor = (block_values.astype(jnp.float32) * block_scales.astype(jnp.float32)[:, :, None]).astype(jnp.bfloat16)
        folded = jnp.einsum('jr,ijk->irk', two_wide, tensor.astype(jnp.float32)).astype(jnp.bfloat16)
        partial_value = jnp.einsum('irk,ks->irs', folded.astype(jnp.float32), chosen_wide)
        return partial_value.reshape(partial_value.shape[0], -1)
    blocks = ALL_ROWS // ROWS_DEV
    partial_value = lax.map(project, (quantized.reshape(blocks, ROWS_DEV, ALL_COLS, SLAB), scales.reshape(blocks, ROWS_DEV, ALL_COLS)))
    partial_value = partial_value.reshape(ALL_ROWS, RANK * RANK)
    flat_core = core_tensor.reshape(RANK, RANK * RANK)
    target = jnp.dot(partial_value, flat_core.T, precision=highest)
    gram_two = jnp.dot(mode_two.T, mode_two, preferred_element_type=jnp.float32)
    gram_three = jnp.dot(chosen.T, chosen, preferred_element_type=jnp.float32)
    coupling = weight_gram(core_tensor, gram_two, gram_three)
    updated = hals_sweep(mode_one, target, coupling)
    spread = jnp.sqrt(lax.optimization_barrier(jnp.sum(updated * updated, axis=0)) / ALL_ROWS + 1e-06)
    return (updated / spread, core_tensor * spread[:, None, None])
```

```python
import functools

import jax
import jax.numpy as jnp
from jax import lax
from jax.experimental import pallas as pl
from jax.experimental.pallas import tpu as pltpu
from jax.sharding import PartitionSpec as P

SLAB = 128
GROUP = 8
STEP = 32
MESH = pl.DeviceIdType.MESH
HIGHEST = lax.Precision.HIGHEST
NT = (((1,), (1,)), ((), ()))
TN = (((0,), (0,)), ((), ()))


def swap_blocks(parts):
    axis = parts[0].ndim - 1
    lane = lax.broadcasted_iota(jnp.int32, parts[0].shape, axis)
    for bit, shift in ((1, 32), (2, 64)):
        low = (lane & shift) == 0
        out = [None] * 4
        for b in range(4):
            if b & bit:
                continue
            x, y = parts[b], parts[b | bit]
            out[b] = jnp.where(low, x, pltpu.roll(y, shift, axis))
            out[b | bit] = jnp.where(low, pltpu.roll(x, 128 - shift, axis), y)
        parts = out
    return parts


def kernel(
    n_rows, n_cols, slab_ref, q_hbm, scales_ref, one_ref, two_ref, three_ref, core_ref,
    new_one_ref, new_core_ref,
    q_ref, bd_ref, pick_ref, pf_ref, cf_ref, yf_ref, gram_ref, target_ref, square_ref,
    q_sem, core_send, core_recv, gram_send, gram_recv, target_send, target_recv, sq_send, sq_recv,
):
    row, col = lax.axis_index("rows"), lax.axis_index("cols")
    n_i, n_j = scales_ref.shape
    own = core_ref.shape[0]
    rank = two_ref.shape[0]
    chunks = n_i // STEP
    wide = GROUP * rank

    def chunk_copy(c):
        rows = pl.ds(pl.multiple_of(c * STEP, STEP), STEP)
        return pltpu.make_async_copy(q_hbm.at[rows], q_ref.at[rows], q_sem.at[c])

    for c in range(chunks):
        chunk_copy(c).start()

    barrier = pltpu.get_barrier_semaphore()
    for d in range(1, n_rows):
        pl.semaphore_signal(
            barrier, inc=1, device_id={"rows": lax.rem(row + d, n_rows), "cols": col}, device_id_type=MESH
        )
    for d in range(1, n_cols):
        pl.semaphore_signal(
            barrier, inc=1, device_id={"rows": row, "cols": lax.rem(col + d, n_cols)}, device_id_type=MESH
        )

    def push(ref, size, send, recv, axis, d):
        count, me = (n_rows, row) if axis == "rows" else (n_cols, col)
        peer = lax.rem(me + d, count)
        where = {"rows": peer, "cols": col} if axis == "rows" else {"rows": row, "cols": peer}
        slot = ref.at[pl.ds(pl.multiple_of(me * size, size), size), :]
        return pltpu.make_async_remote_copy(
            src_ref=slot, dst_ref=slot, send_sem=send.at[d], recv_sem=recv.at[d], device_id=where, device_id_type=MESH
        )

    wanted = jnp.full((rank, SLAB), slab_ref[0], jnp.int32)
    chosen_t = jnp.zeros((rank, SLAB), jnp.float32)
    for n in range(three_ref.shape[1] // SLAB):
        piece = three_ref[:, n * SLAB : (n + 1) * SLAB].astype(jnp.float32)
        chosen_t = jnp.where(wanted == n, piece, chosen_t)
    chosen = chosen_t.T.astype(jnp.bfloat16)
    chosen_t = chosen_t.astype(jnp.bfloat16)
    two = two_ref[...]
    tiled = jnp.concatenate([chosen] * GROUP, axis=1)
    block = lax.broadcasted_iota(jnp.int32, tiled.shape, 1) // rank
    for t in range(GROUP):
        bd_ref[t * SLAB : (t + 1) * SLAB, :] = jnp.where(block == t, tiled, jnp.zeros_like(tiled))
    which = lax.broadcasted_iota(jnp.int32, pick_ref.shape, 1) // rank
    pick_ref[...] = jnp.where(
        which == lax.broadcasted_iota(jnp.int32, pick_ref.shape, 0), 1.0, 0.0
    ).astype(jnp.bfloat16)
    for q in range(own):
        packed = jnp.concatenate([core_ref[q, 8 * b : 8 * b + 8, :] for b in range(4)], axis=1)
        cf_ref[pl.ds(pl.multiple_of((row * own + q) * 8, 8), 8), :] = packed
    gram = lax.dot_general(two, two, NT, preferred_element_type=jnp.float32)
    gram_ref[pl.ds(pl.multiple_of(col * rank, rank), rank), :] = gram

    pl.semaphore_wait(barrier, n_rows + n_cols - 2)
    cores = [push(cf_ref, 8 * own, core_send, core_recv, "rows", d) for d in range(1, n_rows)]
    grams = [push(gram_ref, rank, gram_send, gram_recv, "cols", d) for d in range(1, n_cols)]
    for copy in grams + cores:
        copy.start()

    def chunk(c, carry):
        chunk_copy(c).wait()
        base = pl.multiple_of(c * STEP, STEP)
        spread_scales = lax.dot_general(
            scales_ref[pl.ds(base, STEP), :], pick_ref[...], TN, preferred_element_type=jnp.float32
        )
        lhs = jnp.concatenate(
            [
                jnp.concatenate([q_ref[base + g * GROUP + t] for t in range(GROUP)], axis=1)
                for g in range(STEP // GROUP)
            ],
            axis=0,
        )
        projected = jnp.dot(lhs, bd_ref[...], preferred_element_type=jnp.float32)
        for g in range(STEP // GROUP):
            scaled = projected[g * n_j : (g + 1) * n_j] * spread_scales[:, g * wide : (g + 1) * wide]
            partial = jnp.dot(two, scaled.astype(jnp.bfloat16), preferred_element_type=jnp.float32)
            for h in range(wide // 128):
                turned = swap_blocks([partial[8 * b : 8 * b + 8, 128 * h : 128 * h + 128] for b in range(4)])
                start = pl.multiple_of((base + g * GROUP + 4 * h) * 8, 32)
                pf_ref[pl.ds(start, 32), :] = jnp.concatenate(turned, axis=0)
        return carry

    lax.fori_loop(0, chunks, chunk, 0)

    for copy in cores:
        copy.wait_recv()

    def flat(ref, count):
        return jnp.concatenate([ref[pl.ds(a, count, stride=8), :] for a in range(8)], axis=1)

    core_flat = flat(cf_ref, rank)
    target_ref[pl.ds(pl.multiple_of(col * rank, rank), rank), :] = lax.dot_general(
        core_flat, flat(pf_ref, n_i), NT, preferred_element_type=jnp.float32, precision=HIGHEST
    )
    targets = [push(target_ref, rank, target_send, target_recv, "cols", d) for d in range(1, n_cols)]
    for copy in targets:
        copy.start()

    quad = jnp.concatenate([chosen_t] * 4, axis=0)
    gram_three = lax.dot_general(quad, quad, NT, preferred_element_type=jnp.float32)
    same = lax.broadcasted_iota(jnp.int32, gram_three.shape, 0) // rank == (
        lax.broadcasted_iota(jnp.int32, gram_three.shape, 1) // rank
    )
    gram_three = jnp.where(same, gram_three, 0.0)
    for copy in grams:
        copy.wait_recv()
    gram_two = sum(gram_ref[c * rank : (c + 1) * rank, :] for c in range(1, n_cols)) + gram_ref[0:rank, :]
    left = jnp.dot(cf_ref[...], gram_three, preferred_element_type=jnp.float32, precision=HIGHEST)
    stacked = []
    for g in range(rank // 4):
        stacked.append(
            jnp.concatenate(swap_blocks([left[32 * g + 8 * t : 32 * g + 8 * t + 8] for t in range(4)]), axis=0)
        )
    left = jnp.dot(
        gram_two, jnp.concatenate(stacked, axis=1), preferred_element_type=jnp.float32, precision=HIGHEST
    )
    for g in range(rank // 4):
        back = swap_blocks([left[8 * b : 8 * b + 8, 128 * g : 128 * g + 128] for b in range(4)])
        yf_ref[32 * g : 32 * g + 32, :] = jnp.concatenate(back, axis=0)
    coupling = lax.dot_general(
        flat(yf_ref, rank), core_flat, NT, preferred_element_type=jnp.float32, precision=HIGHEST
    )
    diagonal = lax.broadcasted_iota(jnp.int32, coupling.shape, 0) == lax.broadcasted_iota(jnp.int32, coupling.shape, 1)
    inverse = 1.0 / jnp.sum(jnp.where(diagonal, coupling, 0.0), axis=1, keepdims=True)
    current = one_ref[...]
    fitted = jnp.dot(coupling, current, preferred_element_type=jnp.float32, precision=HIGHEST)
    weights = coupling * inverse

    for copy in targets:
        copy.wait_recv()
    target = target_ref[0:rank, :]
    for c in range(1, n_cols):
        target = target + target_ref[c * rank : (c + 1) * rank, :]
    residual = (target - fitted) * inverse

    tiles = [residual[8 * b : 8 * b + 8] for b in range(rank // 8)]
    changes = []
    for q in range(rank):
        b, a = divmod(q, 8)
        change = jnp.maximum(tiles[b][a : a + 1], -current[q : q + 1])
        changes.append(change)
        for k in range(b, rank // 8):
            tiles[k] = tiles[k] - weights[8 * k : 8 * k + 8, q : q + 1] * change
    updated = jnp.maximum(current + jnp.concatenate(changes, axis=0), 0.0)

    squares = jnp.sum(updated * updated, axis=1, keepdims=True)
    lane = lax.broadcasted_iota(jnp.int32, (8, 128), 1)
    packed = jnp.zeros((8, 128), jnp.float32)
    for b in range(rank // 8):
        packed = jnp.where(lane == b, squares[8 * b : 8 * b + 8], packed)
    square_ref[pl.ds(pl.multiple_of(row * 8, 8), 8), :] = packed
    sums = [push(square_ref, 8, sq_send, sq_recv, "rows", d) for d in range(1, n_rows)]
    for copy in sums:
        copy.start()
    for copy in sums:
        copy.wait_recv()
    totals = square_ref[0:8, :]
    for r in range(1, n_rows):
        totals = totals + square_ref[8 * r : 8 * r + 8, :]
    spread = jnp.sqrt(totals / (n_i * n_rows) + 1e-06)
    for b in range(rank // 8):
        new_one_ref[8 * b : 8 * b + 8, :] = updated[8 * b : 8 * b + 8] / spread[:, b : b + 1]
    place = lax.broadcasted_iota(jnp.int32, (8, 128), 0) + 8 * lane
    for q in range(own):
        mine = jnp.where(place == row * own + q, spread, 0.0)
        mine = jnp.sum(jnp.sum(mine, axis=1, keepdims=True), axis=0, keepdims=True)
        new_core_ref[q] = core_ref[q] * mine
    for copy in cores + grams + targets + sums:
        copy.wait_send()


def local(n_rows, n_cols, quantized, scales, mode_one, mode_two, mode_three, core_tensor, slab_index):
    n_i, n_j, _ = quantized.shape
    rank = mode_two.shape[1]
    own = core_tensor.shape[0]
    f32, bf16 = jnp.float32, jnp.bfloat16
    vmem = pl.BlockSpec(memory_space=pltpu.VMEM)
    dma = pltpu.SemaphoreType.DMA
    one_t, new_core = pl.pallas_call(
        functools.partial(kernel, n_rows, n_cols),
        out_shape=(
            jax.ShapeDtypeStruct((rank, n_i), f32),
            jax.ShapeDtypeStruct((own, rank, rank), f32),
        ),
        in_specs=[pl.BlockSpec(memory_space=pltpu.SMEM), pl.BlockSpec(memory_space=pl.ANY)] + [vmem] * 5,
        out_specs=(vmem, vmem),
        scratch_shapes=[
            pltpu.VMEM(quantized.shape, bf16),
            pltpu.VMEM((GROUP * SLAB, GROUP * rank), bf16),
            pltpu.VMEM((STEP, STEP * rank), bf16),
            pltpu.VMEM((n_i * 8, 128), f32),
            pltpu.VMEM((rank * 8, 128), f32),
            pltpu.VMEM((rank * 8, 128), f32),
            pltpu.VMEM((n_cols * rank, rank), f32),
            pltpu.VMEM((n_cols * rank, n_i), f32),
            pltpu.VMEM((n_rows * 8, 128), f32),
            dma((n_i // STEP,)),
            dma((n_rows,)),
            dma((n_rows,)),
            dma((n_cols,)),
            dma((n_cols,)),
            dma((n_cols,)),
            dma((n_cols,)),
            dma((n_rows,)),
            dma((n_rows,)),
        ],
        compiler_params=pltpu.CompilerParams(
            collective_id=0, has_side_effects=True, vmem_limit_bytes=40 * 1024 * 1024
        ),
    )(slab_index, quantized, scales, mode_one.T, mode_two.T, mode_three.T, core_tensor)
    return one_t.T, new_core


def solution(mesh):
    in_specs = (
        P("rows", "cols", None),
        P("rows", "cols"),
        P("rows", None),
        P("cols", None),
        P(),
        P("rows", None, None),
        P(),
    )
    out_specs = (P("rows", None), P("rows", None, None))
    return jax.shard_map(
        functools.partial(local, mesh.shape["rows"], mesh.shape["cols"]),
        mesh=mesh,
        in_specs=in_specs,
        out_specs=out_specs,
        check_vma=False,
    )
```

```python
import functools

import jax
import jax.numpy as jnp
from jax import lax
from jax.experimental import pallas as pl
from jax.experimental.pallas import tpu as pltpu
from jax.sharding import PartitionSpec as P

SLAB = 128
GROUP = 8
STEP = 32
MESH = pl.DeviceIdType.MESH
HIGHEST = lax.Precision.HIGHEST
NT = (((1,), (1,)), ((), ()))
TN = (((0,), (0,)), ((), ()))


def swap_blocks(parts):
    axis = parts[0].ndim - 1
    lane = lax.broadcasted_iota(jnp.int32, parts[0].shape, axis)
    for bit, shift in ((1, 32), (2, 64)):
        low = (lane & shift) == 0
        out = [None] * 4
        for b in range(4):
            if b & bit:
                continue
            x, y = parts[b], parts[b | bit]
            out[b] = jnp.where(low, x, pltpu.roll(y, shift, axis))
            out[b | bit] = jnp.where(low, pltpu.roll(x, 128 - shift, axis), y)
        parts = out
    return parts


def kernel(
    n_rows, n_cols, slab_ref, q_hbm, scales_hbm, one_hbm, two_hbm, three_hbm, core_hbm,
    new_one_ref, new_core_ref,
    scales_ref, one_ref, two_ref, three_ref, core_ref, q_ref, bd_ref, pick_ref, pf_ref, cf_ref, yf_ref, gram_ref, target_ref, square_ref,
    in_sem, q_sem, core_send, core_recv, gram_send, gram_recv, target_send, target_recv, sq_send, sq_recv,
):
    row, col = lax.axis_index("rows"), lax.axis_index("cols")
    n_i, n_j = scales_ref.shape
    own = core_ref.shape[0]
    rank = two_ref.shape[0]
    chunks = n_i // STEP
    wide = GROUP * rank

    def chunk_copy(c):
        rows = pl.ds(pl.multiple_of(c * STEP, STEP), STEP)
        return pltpu.make_async_copy(q_hbm.at[rows], q_ref.at[rows], q_sem.at[c])

    barrier = pltpu.get_barrier_semaphore()
    for d in range(1, n_rows):
        pl.semaphore_signal(
            barrier, inc=1, device_id={"rows": lax.rem(row + d, n_rows), "cols": col}, device_id_type=MESH
        )
    for d in range(1, n_cols):
        pl.semaphore_signal(
            barrier, inc=1, device_id={"rows": row, "cols": lax.rem(col + d, n_cols)}, device_id_type=MESH
        )

    small = [
        pltpu.make_async_copy(src, dst, in_sem.at[n])
        for n, (src, dst) in enumerate(
            (
                (core_hbm, core_ref),
                (three_hbm, three_ref),
                (two_hbm, two_ref),
                (scales_hbm, scales_ref),
                (one_hbm, one_ref),
            )
        )
    ]
    for copy in small:
        copy.start()
    for c in range(chunks):
        chunk_copy(c).start()

    def push(ref, size, send, recv, axis, d):
        count, me = (n_rows, row) if axis == "rows" else (n_cols, col)
        peer = lax.rem(me + d, count)
        where = {"rows": peer, "cols": col} if axis == "rows" else {"rows": row, "cols": peer}
        slot = ref.at[pl.ds(pl.multiple_of(me * size, size), size), :]
        return pltpu.make_async_remote_copy(
            src_ref=slot, dst_ref=slot, send_sem=send.at[d], recv_sem=recv.at[d], device_id=where, device_id_type=MESH
        )

    which = lax.broadcasted_iota(jnp.int32, pick_ref.shape, 1) // rank
    pick_ref[...] = jnp.where(
        which == lax.broadcasted_iota(jnp.int32, pick_ref.shape, 0), 1.0, 0.0
    ).astype(jnp.bfloat16)
    small[0].wait()
    for q in range(own):
        packed = jnp.concatenate([core_ref[q, 8 * b : 8 * b + 8, :] for b in range(4)], axis=1)
        cf_ref[pl.ds(pl.multiple_of((row * own + q) * 8, 8), 8), :] = packed
    for copy in small[1:]:
        copy.wait()
    wanted = jnp.full((rank, SLAB), slab_ref[0], jnp.int32)
    chosen_t = jnp.zeros((rank, SLAB), jnp.float32)
    for n in range(three_ref.shape[1] // SLAB):
        piece = three_ref[:, n * SLAB : (n + 1) * SLAB].astype(jnp.float32)
        chosen_t = jnp.where(wanted == n, piece, chosen_t)
    chosen = chosen_t.T.astype(jnp.bfloat16)
    chosen_t = chosen_t.astype(jnp.bfloat16)
    two = two_ref[...]
    tiled = jnp.concatenate([chosen] * GROUP, axis=1)
    block = lax.broadcasted_iota(jnp.int32, tiled.shape, 1) // rank
    for t in range(GROUP):
        bd_ref[t * SLAB : (t + 1) * SLAB, :] = jnp.where(block == t, tiled, jnp.zeros_like(tiled))
    gram = lax.dot_general(two, two, NT, preferred_element_type=jnp.float32)
    gram_ref[pl.ds(pl.multiple_of(col * rank, rank), rank), :] = gram

    pl.semaphore_wait(barrier, n_rows + n_cols - 2)
    cores = [push(cf_ref, 8 * own, core_send, core_recv, "rows", d) for d in range(1, n_rows)]
    grams = [push(gram_ref, rank, gram_send, gram_recv, "cols", d) for d in range(1, n_cols)]
    for copy in grams + cores:
        copy.start()

    def chunk(c, carry):
        chunk_copy(c).wait()
        base = pl.multiple_of(c * STEP, STEP)
        spread_scales = lax.dot_general(
            scales_ref[pl.ds(base, STEP), :], pick_ref[...], TN, preferred_element_type=jnp.float32
        )
        lhs = jnp.concatenate(
            [
                jnp.concatenate([q_ref[base + g * GROUP + t] for t in range(GROUP)], axis=1)
                for g in range(STEP // GROUP)
            ],
            axis=0,
        )
        projected = jnp.dot(lhs, bd_ref[...], preferred_element_type=jnp.float32)
        for g in range(STEP // GROUP):
            scaled = projected[g * n_j : (g + 1) * n_j] * spread_scales[:, g * wide : (g + 1) * wide]
            partial = jnp.dot(two, scaled.astype(jnp.bfloat16), preferred_element_type=jnp.float32)
            for h in range(wide // 128):
                turned = swap_blocks([partial[8 * b : 8 * b + 8, 128 * h : 128 * h + 128] for b in range(4)])
                start = pl.multiple_of((base + g * GROUP + 4 * h) * 8, 32)
                pf_ref[pl.ds(start, 32), :] = jnp.concatenate(turned, axis=0)
        return carry

    lax.fori_loop(0, chunks, chunk, 0)

    for copy in cores:
        copy.wait_recv()

    def flat(ref, count):
        return jnp.concatenate([ref[pl.ds(a, count, stride=8), :] for a in range(8)], axis=1)

    core_flat = flat(cf_ref, rank)
    target_ref[pl.ds(pl.multiple_of(col * rank, rank), rank), :] = lax.dot_general(
        core_flat, flat(pf_ref, n_i), NT, preferred_element_type=jnp.float32, precision=HIGHEST
    )
    targets = [push(target_ref, rank, target_send, target_recv, "cols", d) for d in range(1, n_cols)]
    for copy in targets:
        copy.start()

    quad = jnp.concatenate([chosen_t] * 4, axis=0)
    gram_three = lax.dot_general(quad, quad, NT, preferred_element_type=jnp.float32)
    same = lax.broadcasted_iota(jnp.int32, gram_three.shape, 0) // rank == (
        lax.broadcasted_iota(jnp.int32, gram_three.shape, 1) // rank
    )
    gram_three = jnp.where(same, gram_three, 0.0)
    for copy in grams:
        copy.wait_recv()
    gram_two = sum(gram_ref[c * rank : (c + 1) * rank, :] for c in range(1, n_cols)) + gram_ref[0:rank, :]
    left = jnp.dot(cf_ref[...], gram_three, preferred_element_type=jnp.float32, precision=HIGHEST)
    stacked = []
    for g in range(rank // 4):
        stacked.append(
            jnp.concatenate(swap_blocks([left[32 * g + 8 * t : 32 * g + 8 * t + 8] for t in range(4)]), axis=0)
        )
    left = jnp.dot(
        gram_two, jnp.concatenate(stacked, axis=1), preferred_element_type=jnp.float32, precision=HIGHEST
    )
    for g in range(rank // 4):
        back = swap_blocks([left[8 * b : 8 * b + 8, 128 * g : 128 * g + 128] for b in range(4)])
        yf_ref[32 * g : 32 * g + 32, :] = jnp.concatenate(back, axis=0)
    coupling = lax.dot_general(
        flat(yf_ref, rank), core_flat, NT, preferred_element_type=jnp.float32, precision=HIGHEST
    )
    diagonal = lax.broadcasted_iota(jnp.int32, coupling.shape, 0) == lax.broadcasted_iota(jnp.int32, coupling.shape, 1)
    inverse = 1.0 / jnp.sum(jnp.where(diagonal, coupling, 0.0), axis=1, keepdims=True)
    current = one_ref[...]
    fitted = jnp.dot(coupling, current, preferred_element_type=jnp.float32, precision=HIGHEST)
    weights = coupling * inverse

    for copy in targets:
        copy.wait_recv()
    target = target_ref[0:rank, :]
    for c in range(1, n_cols):
        target = target + target_ref[c * rank : (c + 1) * rank, :]
    residual = (target - fitted) * inverse

    tiles = [residual[8 * b : 8 * b + 8] for b in range(rank // 8)]
    changes = []
    for q in range(rank):
        b, a = divmod(q, 8)
        change = jnp.maximum(tiles[b][a : a + 1], -current[q : q + 1])
        changes.append(change)
        for k in range(b, rank // 8):
            tiles[k] = tiles[k] - weights[8 * k : 8 * k + 8, q : q + 1] * change
    updated = jnp.maximum(current + jnp.concatenate(changes, axis=0), 0.0)

    squares = jnp.sum(updated * updated, axis=1, keepdims=True)
    lane = lax.broadcasted_iota(jnp.int32, (8, 128), 1)
    packed = jnp.zeros((8, 128), jnp.float32)
    for b in range(rank // 8):
        packed = jnp.where(lane == b, squares[8 * b : 8 * b + 8], packed)
    square_ref[pl.ds(pl.multiple_of(row * 8, 8), 8), :] = packed
    sums = [push(square_ref, 8, sq_send, sq_recv, "rows", d) for d in range(1, n_rows)]
    for copy in sums:
        copy.start()
    for copy in sums:
        copy.wait_recv()
    totals = square_ref[0:8, :]
    for r in range(1, n_rows):
        totals = totals + square_ref[8 * r : 8 * r + 8, :]
    spread = jnp.sqrt(totals / (n_i * n_rows) + 1e-06)
    for b in range(rank // 8):
        new_one_ref[8 * b : 8 * b + 8, :] = updated[8 * b : 8 * b + 8] / spread[:, b : b + 1]
    place = lax.broadcasted_iota(jnp.int32, (8, 128), 0) + 8 * lane
    for q in range(own):
        mine = jnp.where(place == row * own + q, spread, 0.0)
        mine = jnp.sum(jnp.sum(mine, axis=1, keepdims=True), axis=0, keepdims=True)
        new_core_ref[q] = core_ref[q] * mine
    for copy in cores + grams + targets + sums:
        copy.wait_send()


def local(n_rows, n_cols, quantized, scales, mode_one, mode_two, mode_three, core_tensor, slab_index):
    n_i, n_j, _ = quantized.shape
    rank = mode_two.shape[1]
    own = core_tensor.shape[0]
    f32, bf16 = jnp.float32, jnp.bfloat16
    vmem = pl.BlockSpec(memory_space=pltpu.VMEM)
    dma = pltpu.SemaphoreType.DMA
    one_t, new_core = pl.pallas_call(
        functools.partial(kernel, n_rows, n_cols),
        out_shape=(
            jax.ShapeDtypeStruct((rank, n_i), f32),
            jax.ShapeDtypeStruct((own, rank, rank), f32),
        ),
        in_specs=[pl.BlockSpec(memory_space=pltpu.SMEM)] + [pl.BlockSpec(memory_space=pl.ANY)] * 6,
        out_specs=(vmem, vmem),
        scratch_shapes=[
            pltpu.VMEM(scales.shape, bf16),
            pltpu.VMEM((rank, n_i), f32),
            pltpu.VMEM((rank, n_j), bf16),
            pltpu.VMEM((rank, mode_three.shape[0]), bf16),
            pltpu.VMEM(core_tensor.shape, f32),
            pltpu.VMEM(quantized.shape, bf16),
            pltpu.VMEM((GROUP * SLAB, GROUP * rank), bf16),
            pltpu.VMEM((STEP, STEP * rank), bf16),
            pltpu.VMEM((n_i * 8, 128), f32),
            pltpu.VMEM((rank * 8, 128), f32),
            pltpu.VMEM((rank * 8, 128), f32),
            pltpu.VMEM((n_cols * rank, rank), f32),
            pltpu.VMEM((n_cols * rank, n_i), f32),
            pltpu.VMEM((n_rows * 8, 128), f32),
            dma((5,)),
            dma((n_i // STEP,)),
            dma((n_rows,)),
            dma((n_rows,)),
            dma((n_cols,)),
            dma((n_cols,)),
            dma((n_cols,)),
            dma((n_cols,)),
            dma((n_rows,)),
            dma((n_rows,)),
        ],
        compiler_params=pltpu.CompilerParams(
            collective_id=0, has_side_effects=True, vmem_limit_bytes=64 * 1024 * 1024
        ),
    )(slab_index, quantized, scales, mode_one.T, mode_two.T, mode_three.T, core_tensor)
    return one_t.T, new_core


def solution(mesh):
    in_specs = (
        P("rows", "cols", None),
        P("rows", "cols"),
        P("rows", None),
        P("cols", None),
        P(),
        P("rows", None, None),
        P(),
    )
    out_specs = (P("rows", None), P("rows", None, None))
    return jax.shard_map(
        functools.partial(local, mesh.shape["rows"], mesh.shape["cols"]),
        mesh=mesh,
        in_specs=in_specs,
        out_specs=out_specs,
        check_vma=False,
    )
```

```python
import functools

import jax
import jax.numpy as jnp
from jax import lax
from jax.experimental import pallas as pl
from jax.experimental.pallas import tpu as pltpu
from jax.sharding import PartitionSpec as P

SLAB = 128
GROUP = 8
STEP = 32
MESH = pl.DeviceIdType.MESH
HIGHEST = lax.Precision.HIGHEST
NT = (((1,), (1,)), ((), ()))
TN = (((0,), (0,)), ((), ()))


def swap_blocks(parts):
    axis = parts[0].ndim - 1
    lane = lax.broadcasted_iota(jnp.int32, parts[0].shape, axis)
    for bit, shift in ((1, 32), (2, 64)):
        low = (lane & shift) == 0
        out = [None] * 4
        for b in range(4):
            if b & bit:
                continue
            x, y = parts[b], parts[b | bit]
            out[b] = jnp.where(low, x, pltpu.roll(y, shift, axis))
            out[b | bit] = jnp.where(low, pltpu.roll(x, 128 - shift, axis), y)
        parts = out
    return parts


def flip(index, bit):
    return index + bit - 2 * bit * lax.rem(index // bit, 2)


def kernel(
    n_rows, n_cols, slab_ref, q_hbm, scales_hbm, one_hbm, two_hbm, three_hbm, core_hbm,
    new_one_ref, new_core_ref,
    scales_ref, one_ref, two_ref, three_ref, core_ref, q_ref, bd_ref, pick_ref, pf_ref, cf_ref, core_all_ref, yf_ref, gram_ref, target_ref, square_ref,
    in_sem, q_sem, core_send, core_recv, gram_send, gram_recv, target_send, target_recv, sq_send, sq_recv,
):
    row, col = lax.axis_index("rows"), lax.axis_index("cols")
    n_i, n_j = scales_ref.shape
    own = core_ref.shape[0]
    rank = two_ref.shape[0]
    bits = [n_rows >> (k + 1) for k in range(n_rows.bit_length() - 1)]
    chunks = n_i // STEP
    wide = GROUP * rank

    def chunk_copy(c):
        rows = pl.ds(pl.multiple_of(c * STEP, STEP), STEP)
        return pltpu.make_async_copy(q_hbm.at[rows], q_ref.at[rows], q_sem.at[c])

    barrier = pltpu.get_barrier_semaphore()
    for bit in bits:
        pl.semaphore_signal(barrier, inc=1, device_id={"rows": flip(row, bit), "cols": col}, device_id_type=MESH)
    for d in range(1, n_cols):
        pl.semaphore_signal(
            barrier, inc=1, device_id={"rows": row, "cols": lax.rem(col + d, n_cols)}, device_id_type=MESH
        )

    small = [
        pltpu.make_async_copy(src, dst, in_sem.at[n])
        for n, (src, dst) in enumerate(
            (
                (core_hbm, core_ref),
                (three_hbm, three_ref),
                (two_hbm, two_ref),
                (scales_hbm, scales_ref),
                (one_hbm, one_ref),
            )
        )
    ]
    for copy in small:
        copy.start()
    for c in range(chunks):
        chunk_copy(c).start()

    def push(ref, size, send, recv, d):
        where = {"rows": row, "cols": lax.rem(col + d, n_cols)}
        slot = ref.at[pl.ds(pl.multiple_of(col * size, size), size), :]
        return pltpu.make_async_remote_copy(
            src_ref=slot, dst_ref=slot, send_sem=send.at[d], recv_sem=recv.at[d], device_id=where, device_id_type=MESH
        )

    place = sum(lax.rem(row // bit, 2) * (n_rows // 2 // bit) for bit in bits)

    def core_step(k):
        size = (8 * own) << k
        slot = cf_ref.at[pl.ds(pl.multiple_of((place // (1 << k)) * size, size), size), :]
        return pltpu.make_async_remote_copy(
            src_ref=slot, dst_ref=slot, send_sem=core_send.at[k], recv_sem=core_recv.at[k],
            device_id={"rows": flip(row, bits[k]), "cols": col}, device_id_type=MESH,
        )

    which = lax.broadcasted_iota(jnp.int32, pick_ref.shape, 1) // rank
    pick_ref[...] = jnp.where(
        which == lax.broadcasted_iota(jnp.int32, pick_ref.shape, 0), 1.0, 0.0
    ).astype(jnp.bfloat16)
    small[0].wait()
    for q in range(own):
        packed = jnp.concatenate([core_ref[q, 8 * b : 8 * b + 8, :] for b in range(4)], axis=1)
        cf_ref[pl.ds(pl.multiple_of((place * own + q) * 8, 8), 8), :] = packed
    for copy in small[1:]:
        copy.wait()
    wanted = jnp.full((rank, SLAB), slab_ref[0], jnp.int32)
    chosen_t = jnp.zeros((rank, SLAB), jnp.float32)
    for n in range(three_ref.shape[1] // SLAB):
        piece = three_ref[:, n * SLAB : (n + 1) * SLAB].astype(jnp.float32)
        chosen_t = jnp.where(wanted == n, piece, chosen_t)
    chosen = chosen_t.T.astype(jnp.bfloat16)
    chosen_t = chosen_t.astype(jnp.bfloat16)
    two = two_ref[...]
    tiled = jnp.concatenate([chosen] * GROUP, axis=1)
    block = lax.broadcasted_iota(jnp.int32, tiled.shape, 1) // rank
    for t in range(GROUP):
        bd_ref[t * SLAB : (t + 1) * SLAB, :] = jnp.where(block == t, tiled, jnp.zeros_like(tiled))
    gram = lax.dot_general(two, two, NT, preferred_element_type=jnp.float32)
    gram_ref[pl.ds(pl.multiple_of(col * rank, rank), rank), :] = gram

    pl.semaphore_wait(barrier, len(bits) + n_cols - 1)
    grams = [push(gram_ref, rank, gram_send, gram_recv, d) for d in range(1, n_cols)]
    cores = [core_step(k) for k in range(len(bits))]
    cores[0].start()
    for copy in grams:
        copy.start()

    def chunk(c, carry):
        chunk_copy(c).wait()
        base = pl.multiple_of(c * STEP, STEP)
        spread_scales = lax.dot_general(
            scales_ref[pl.ds(base, STEP), :], pick_ref[...], TN, preferred_element_type=jnp.float32
        )
        lhs = jnp.concatenate(
            [
                jnp.concatenate([q_ref[base + g * GROUP + t] for t in range(GROUP)], axis=1)
                for g in range(STEP // GROUP)
            ],
            axis=0,
        )
        projected = jnp.dot(lhs, bd_ref[...], preferred_element_type=jnp.float32)
        for g in range(STEP // GROUP):
            scaled = projected[g * n_j : (g + 1) * n_j] * spread_scales[:, g * wide : (g + 1) * wide]
            partial = jnp.dot(two, scaled.astype(jnp.bfloat16), preferred_element_type=jnp.float32)
            for h in range(wide // 128):
                turned = swap_blocks([partial[8 * b : 8 * b + 8, 128 * h : 128 * h + 128] for b in range(4)])
                start = pl.multiple_of((base + g * GROUP + 4 * h) * 8, 32)
                pf_ref[pl.ds(start, 32), :] = jnp.concatenate(turned, axis=0)
        return carry

    early = min(len(bits) - 1, chunks)
    for c in range(chunks):
        chunk(c, 0)
        if c < early:
            cores[c].wait_recv()
            cores[c + 1].start()
    for k in range(early, len(bits)):
        cores[k].wait_recv()
        if k + 1 < len(bits):
            cores[k + 1].start()
    for r in range(n_rows):
        slot = sum(r // bit % 2 * (n_rows // 2 // bit) for bit in bits)
        core_all_ref[8 * own * r : 8 * own * (r + 1), :] = cf_ref[8 * own * slot : 8 * own * (slot + 1), :]

    def flat(ref, count):
        return jnp.concatenate([ref[pl.ds(a, count, stride=8), :] for a in range(8)], axis=1)

    core_flat = flat(core_all_ref, rank)
    target_ref[pl.ds(pl.multiple_of(col * rank, rank), rank), :] = lax.dot_general(
        core_flat, flat(pf_ref, n_i), NT, preferred_element_type=jnp.float32, precision=HIGHEST
    )
    targets = [push(target_ref, rank, target_send, target_recv, d) for d in range(1, n_cols)]
    for copy in targets:
        copy.start()

    quad = jnp.concatenate([chosen_t] * 4, axis=0)
    gram_three = lax.dot_general(quad, quad, NT, preferred_element_type=jnp.float32)
    same = lax.broadcasted_iota(jnp.int32, gram_three.shape, 0) // rank == (
        lax.broadcasted_iota(jnp.int32, gram_three.shape, 1) // rank
    )
    gram_three = jnp.where(same, gram_three, 0.0)
    for copy in grams:
        copy.wait_recv()
    gram_two = sum(gram_ref[c * rank : (c + 1) * rank, :] for c in range(1, n_cols)) + gram_ref[0:rank, :]
    left = jnp.dot(core_all_ref[...], gram_three, preferred_element_type=jnp.float32, precision=HIGHEST)
    stacked = []
    for g in range(rank // 4):
        stacked.append(
            jnp.concatenate(swap_blocks([left[32 * g + 8 * t : 32 * g + 8 * t + 8] for t in range(4)]), axis=0)
        )
    left = jnp.dot(
        gram_two, jnp.concatenate(stacked, axis=1), preferred_element_type=jnp.float32, precision=HIGHEST
    )
    for g in range(rank // 4):
        back = swap_blocks([left[8 * b : 8 * b + 8, 128 * g : 128 * g + 128] for b in range(4)])
        yf_ref[32 * g : 32 * g + 32, :] = jnp.concatenate(back, axis=0)
    coupling = lax.dot_general(
        flat(yf_ref, rank), core_flat, NT, preferred_element_type=jnp.float32, precision=HIGHEST
    )
    diagonal = lax.broadcasted_iota(jnp.int32, coupling.shape, 0) == lax.broadcasted_iota(jnp.int32, coupling.shape, 1)
    inverse = 1.0 / jnp.sum(jnp.where(diagonal, coupling, 0.0), axis=1, keepdims=True)
    current = one_ref[...]
    fitted = jnp.dot(coupling, current, preferred_element_type=jnp.float32, precision=HIGHEST)
    weights = coupling * inverse

    for copy in targets:
        copy.wait_recv()
    target = target_ref[0:rank, :]
    for c in range(1, n_cols):
        target = target + target_ref[c * rank : (c + 1) * rank, :]
    residual = (target - fitted) * inverse

    tiles = [residual[8 * b : 8 * b + 8] for b in range(rank // 8)]
    changes = []
    for q in range(rank):
        b, a = divmod(q, 8)
        change = jnp.maximum(tiles[b][a : a + 1], -current[q : q + 1])
        changes.append(change)
        for k in range(b, rank // 8):
            tiles[k] = tiles[k] - weights[8 * k : 8 * k + 8, q : q + 1] * change
    updated = jnp.maximum(current + jnp.concatenate(changes, axis=0), 0.0)

    squares = jnp.sum(updated * updated, axis=1, keepdims=True)
    lane = lax.broadcasted_iota(jnp.int32, (8, 128), 1)
    packed = jnp.zeros((8, 128), jnp.float32)
    for b in range(rank // 8):
        packed = jnp.where(lane == b, squares[8 * b : 8 * b + 8], packed)
    sums = []
    for k, bit in enumerate(bits):
        square_ref[k, 0] = packed
        copy = pltpu.make_async_remote_copy(
            src_ref=square_ref.at[k, 0], dst_ref=square_ref.at[k, 1], send_sem=sq_send.at[k], recv_sem=sq_recv.at[k],
            device_id={"rows": flip(row, bit), "cols": col}, device_id_type=MESH,
        )
        copy.start()
        copy.wait_recv()
        packed = packed + square_ref[k, 1]
        sums.append(copy)
    totals = packed
    spread = jnp.sqrt(totals / (n_i * n_rows) + 1e-06)
    for b in range(rank // 8):
        new_one_ref[8 * b : 8 * b + 8, :] = updated[8 * b : 8 * b + 8] / spread[:, b : b + 1]
    index = lax.broadcasted_iota(jnp.int32, (8, 128), 0) + 8 * lane
    for q in range(own):
        mine = jnp.where(index == row * own + q, spread, 0.0)
        mine = jnp.sum(jnp.sum(mine, axis=1, keepdims=True), axis=0, keepdims=True)
        new_core_ref[q] = core_ref[q] * mine
    for copy in cores + grams + targets + sums:
        copy.wait_send()


def local(n_rows, n_cols, quantized, scales, mode_one, mode_two, mode_three, core_tensor, slab_index):
    n_i, n_j, _ = quantized.shape
    rank = mode_two.shape[1]
    own = core_tensor.shape[0]
    f32, bf16 = jnp.float32, jnp.bfloat16
    vmem = pl.BlockSpec(memory_space=pltpu.VMEM)
    dma = pltpu.SemaphoreType.DMA
    one_t, new_core = pl.pallas_call(
        functools.partial(kernel, n_rows, n_cols),
        out_shape=(
            jax.ShapeDtypeStruct((rank, n_i), f32),
            jax.ShapeDtypeStruct((own, rank, rank), f32),
        ),
        in_specs=[pl.BlockSpec(memory_space=pltpu.SMEM)] + [pl.BlockSpec(memory_space=pl.ANY)] * 6,
        out_specs=(vmem, vmem),
        scratch_shapes=[
            pltpu.VMEM(scales.shape, bf16),
            pltpu.VMEM((rank, n_i), f32),
            pltpu.VMEM((rank, n_j), bf16),
            pltpu.VMEM((rank, mode_three.shape[0]), bf16),
            pltpu.VMEM(core_tensor.shape, f32),
            pltpu.VMEM(quantized.shape, bf16),
            pltpu.VMEM((GROUP * SLAB, GROUP * rank), bf16),
            pltpu.VMEM((STEP, STEP * rank), bf16),
            pltpu.VMEM((n_i * 8, 128), f32),
            pltpu.VMEM((rank * 8, 128), f32),
            pltpu.VMEM((rank * 8, 128), f32),
            pltpu.VMEM((rank * 8, 128), f32),
            pltpu.VMEM((n_cols * rank, rank), f32),
            pltpu.VMEM((n_cols * rank, n_i), f32),
            pltpu.VMEM((n_rows.bit_length(), 2, 8, 128), f32),
            dma((5,)),
            dma((n_i // STEP,)),
            dma((n_rows,)),
            dma((n_rows,)),
            dma((n_cols,)),
            dma((n_cols,)),
            dma((n_cols,)),
            dma((n_cols,)),
            dma((n_rows,)),
            dma((n_rows,)),
        ],
        compiler_params=pltpu.CompilerParams(
            collective_id=0, has_side_effects=True, vmem_limit_bytes=40 * 1024 * 1024
        ),
    )(
        slab_index,
        *(
            pltpu.with_memory_space_constraint(x, pltpu.HBM)
            for x in (quantized, scales, mode_one.T, mode_two.T, mode_three.T, core_tensor)
        ),
    )
    return one_t.T, new_core


def solution(mesh):
    in_specs = (
        P("rows", "cols", None),
        P("rows", "cols"),
        P("rows", None),
        P("cols", None),
        P(),
        P("rows", None, None),
        P(),
    )
    out_specs = (P("rows", None), P("rows", None, None))
    return jax.shard_map(
        functools.partial(local, mesh.shape["rows"], mesh.shape["cols"]),
        mesh=mesh,
        in_specs=in_specs,
        out_specs=out_specs,
        check_vma=False,
    )
```

```python
import functools

import jax
import jax.numpy as jnp
from jax import lax
from jax.experimental import pallas as pl
from jax.experimental.pallas import tpu as pltpu
from jax.sharding import PartitionSpec as P

SLAB = 128
GROUP = 8
STEP = 32
MESH = pl.DeviceIdType.MESH
HIGHEST = lax.Precision.HIGHEST
NT = (((1,), (1,)), ((), ()))
TN = (((0,), (0,)), ((), ()))


def swap_blocks(parts):
    axis = parts[0].ndim - 1
    lane = lax.broadcasted_iota(jnp.int32, parts[0].shape, axis)
    for bit, shift in ((1, 32), (2, 64)):
        low = (lane & shift) == 0
        out = [None] * 4
        for b in range(4):
            if b & bit:
                continue
            x, y = parts[b], parts[b | bit]
            out[b] = jnp.where(low, x, pltpu.roll(y, shift, axis))
            out[b | bit] = jnp.where(low, pltpu.roll(x, 128 - shift, axis), y)
        parts = out
    return parts


def kernel(
    n_rows, n_cols, slab_ref, q_hbm, scales_hbm, one_hbm, two_hbm, three_hbm, core_hbm,
    new_one_ref, new_core_ref,
    scales_ref, one_ref, two_ref, three_ref, core_ref, q_ref, bd_ref, pick_ref, pf_ref, cf_ref, yf_ref, gram_ref, target_ref, square_ref,
    in_sem, q_sem, core_send, core_recv, gram_send, gram_recv, target_send, target_recv, sq_send, sq_recv,
):
    row, col = lax.axis_index("rows"), lax.axis_index("cols")
    n_i, n_j = scales_ref.shape
    own = core_ref.shape[0]
    rank = two_ref.shape[0]
    chunks = n_i // STEP
    wide = GROUP * rank

    def chunk_copy(c):
        rows = pl.ds(pl.multiple_of(c * STEP, STEP), STEP)
        return pltpu.make_async_copy(q_hbm.at[rows], q_ref.at[rows], q_sem.at[c])

    barrier = pltpu.get_barrier_semaphore()
    for d in range(1, n_rows):
        pl.semaphore_signal(
            barrier, inc=1, device_id={"rows": lax.rem(row + d, n_rows), "cols": col}, device_id_type=MESH
        )
    for d in range(1, n_cols):
        pl.semaphore_signal(
            barrier, inc=1, device_id={"rows": row, "cols": lax.rem(col + d, n_cols)}, device_id_type=MESH
        )

    small = [
        pltpu.make_async_copy(src, dst, in_sem.at[n])
        for n, (src, dst) in enumerate(
            (
                (core_hbm, core_ref),
                (three_hbm, three_ref),
                (two_hbm, two_ref),
                (scales_hbm, scales_ref),
                (one_hbm, one_ref),
            )
        )
    ]
    for copy in small:
        copy.start()
    for c in range(chunks):
        chunk_copy(c).start()

    def push(ref, size, send, recv, axis, d):
        count, me = (n_rows, row) if axis == "rows" else (n_cols, col)
        peer = lax.rem(me + d, count)
        where = {"rows": peer, "cols": col} if axis == "rows" else {"rows": row, "cols": peer}
        slot = ref.at[pl.ds(pl.multiple_of(me * size, size), size), :]
        return pltpu.make_async_remote_copy(
            src_ref=slot, dst_ref=slot, send_sem=send.at[d], recv_sem=recv.at[d], device_id=where, device_id_type=MESH
        )

    which = lax.broadcasted_iota(jnp.int32, pick_ref.shape, 1) // rank
    pick_ref[...] = jnp.where(
        which == lax.broadcasted_iota(jnp.int32, pick_ref.shape, 0), 1.0, 0.0
    ).astype(jnp.bfloat16)
    small[0].wait()
    for q in range(own):
        packed = jnp.concatenate([core_ref[q, 8 * b : 8 * b + 8, :] for b in range(4)], axis=1)
        cf_ref[pl.ds(pl.multiple_of((row * own + q) * 8, 8), 8), :] = packed
    for copy in small[1:]:
        copy.wait()
    wanted = jnp.full((rank, SLAB), slab_ref[0], jnp.int32)
    chosen_t = jnp.zeros((rank, SLAB), jnp.float32)
    for n in range(three_ref.shape[1] // SLAB):
        piece = three_ref[:, n * SLAB : (n + 1) * SLAB].astype(jnp.float32)
        chosen_t = jnp.where(wanted == n, piece, chosen_t)
    chosen = chosen_t.T.astype(jnp.bfloat16)
    chosen_t = chosen_t.astype(jnp.bfloat16)
    two = two_ref[...]
    tiled = jnp.concatenate([chosen] * GROUP, axis=1)
    block = lax.broadcasted_iota(jnp.int32, tiled.shape, 1) // rank
    for t in range(GROUP):
        bd_ref[t * SLAB : (t + 1) * SLAB, :] = jnp.where(block == t, tiled, jnp.zeros_like(tiled))
    gram = lax.dot_general(two, two, NT, preferred_element_type=jnp.float32)
    gram_ref[pl.ds(pl.multiple_of(col * rank, rank), rank), :] = gram

    pl.semaphore_wait(barrier, n_rows + n_cols - 2)
    cores = [push(cf_ref, 8 * own, core_send, core_recv, "rows", d) for d in range(1, n_rows)]
    grams = [push(gram_ref, rank, gram_send, gram_recv, "cols", d) for d in range(1, n_cols)]
    for copy in grams + cores:
        copy.start()

    def chunk(c, carry):
        chunk_copy(c).wait()
        base = pl.multiple_of(c * STEP, STEP)
        spread_scales = lax.dot_general(
            scales_ref[pl.ds(base, STEP), :], pick_ref[...], TN, preferred_element_type=jnp.float32
        )
        lhs = jnp.concatenate(
            [
                jnp.concatenate([q_ref[base + g * GROUP + t] for t in range(GROUP)], axis=1)
                for g in range(STEP // GROUP)
            ],
            axis=0,
        )
        projected = jnp.dot(lhs, bd_ref[...], preferred_element_type=jnp.float32)
        for g in range(STEP // GROUP):
            scaled = projected[g * n_j : (g + 1) * n_j] * spread_scales[:, g * wide : (g + 1) * wide]
            partial = jnp.dot(two, scaled.astype(jnp.bfloat16), preferred_element_type=jnp.float32)
            for h in range(wide // 128):
                turned = swap_blocks([partial[8 * b : 8 * b + 8, 128 * h : 128 * h + 128] for b in range(4)])
                start = pl.multiple_of((base + g * GROUP + 4 * h) * 8, 32)
                pf_ref[pl.ds(start, 32), :] = jnp.concatenate(turned, axis=0)
        return carry

    lax.fori_loop(0, chunks, chunk, 0)

    for copy in cores:
        copy.wait_recv()

    def flat(ref, count):
        return jnp.concatenate([ref[pl.ds(a, count, stride=8), :] for a in range(8)], axis=1)

    core_flat = flat(cf_ref, rank)
    target_ref[pl.ds(pl.multiple_of(col * rank, rank), rank), :] = lax.dot_general(
        core_flat, flat(pf_ref, n_i), NT, preferred_element_type=jnp.float32, precision=HIGHEST
    )
    targets = [push(target_ref, rank, target_send, target_recv, "cols", d) for d in range(1, n_cols)]
    for copy in targets:
        copy.start()

    quad = jnp.concatenate([chosen_t] * 4, axis=0)
    gram_three = lax.dot_general(quad, quad, NT, preferred_element_type=jnp.float32)
    same = lax.broadcasted_iota(jnp.int32, gram_three.shape, 0) // rank == (
        lax.broadcasted_iota(jnp.int32, gram_three.shape, 1) // rank
    )
    gram_three = jnp.where(same, gram_three, 0.0)
    for copy in grams:
        copy.wait_recv()
    gram_two = sum(gram_ref[c * rank : (c + 1) * rank, :] for c in range(1, n_cols)) + gram_ref[0:rank, :]
    left = jnp.dot(cf_ref[...], gram_three, preferred_element_type=jnp.float32, precision=HIGHEST)
    stacked = []
    for g in range(rank // 4):
        stacked.append(
            jnp.concatenate(swap_blocks([left[32 * g + 8 * t : 32 * g + 8 * t + 8] for t in range(4)]), axis=0)
        )
    left = jnp.dot(
        gram_two, jnp.concatenate(stacked, axis=1), preferred_element_type=jnp.float32, precision=HIGHEST
    )
    for g in range(rank // 4):
        back = swap_blocks([left[8 * b : 8 * b + 8, 128 * g : 128 * g + 128] for b in range(4)])
        yf_ref[32 * g : 32 * g + 32, :] = jnp.concatenate(back, axis=0)
    coupling = lax.dot_general(
        flat(yf_ref, rank), core_flat, NT, preferred_element_type=jnp.float32, precision=HIGHEST
    )
    diagonal = lax.broadcasted_iota(jnp.int32, coupling.shape, 0) == lax.broadcasted_iota(jnp.int32, coupling.shape, 1)
    inverse = 1.0 / jnp.sum(jnp.where(diagonal, coupling, 0.0), axis=1, keepdims=True)
    current = one_ref[...]
    fitted = jnp.dot(coupling, current, preferred_element_type=jnp.float32, precision=HIGHEST)
    weights = coupling * inverse

    for copy in targets:
        copy.wait_recv()
    target = target_ref[0:rank, :]
    for c in range(1, n_cols):
        target = target + target_ref[c * rank : (c + 1) * rank, :]
    residual = (target - fitted) * inverse

    tiles = [residual[8 * b : 8 * b + 8] for b in range(rank // 8)]
    changes = []
    for q in range(rank):
        b, a = divmod(q, 8)
        change = jnp.maximum(tiles[b][a : a + 1], -current[q : q + 1])
        changes.append(change)
        for k in range(b, rank // 8):
            tiles[k] = tiles[k] - weights[8 * k : 8 * k + 8, q : q + 1] * change
    updated = jnp.maximum(current + jnp.concatenate(changes, axis=0), 0.0)

    squares = jnp.sum(updated * updated, axis=1, keepdims=True)
    lane = lax.broadcasted_iota(jnp.int32, (8, 128), 1)
    packed = jnp.zeros((8, 128), jnp.float32)
    for b in range(rank // 8):
        packed = jnp.where(lane == b, squares[8 * b : 8 * b + 8], packed)
    square_ref[pl.ds(pl.multiple_of(row * 8, 8), 8), :] = packed
    sums = [push(square_ref, 8, sq_send, sq_recv, "rows", d) for d in range(1, n_rows)]
    for copy in sums:
        copy.start()
    for copy in sums:
        copy.wait_recv()
    totals = square_ref[0:8, :]
    for r in range(1, n_rows):
        totals = totals + square_ref[8 * r : 8 * r + 8, :]
    spread = jnp.sqrt(totals / (n_i * n_rows) + 1e-06)
    for b in range(rank // 8):
        new_one_ref[8 * b : 8 * b + 8, :] = updated[8 * b : 8 * b + 8] / spread[:, b : b + 1]
    place = lax.broadcasted_iota(jnp.int32, (8, 128), 0) + 8 * lane
    for q in range(own):
        mine = jnp.where(place == row * own + q, spread, 0.0)
        mine = jnp.sum(jnp.sum(mine, axis=1, keepdims=True), axis=0, keepdims=True)
        new_core_ref[q] = core_ref[q] * mine
    for copy in cores + grams + targets + sums:
        copy.wait_send()


def local(n_rows, n_cols, quantized, scales, mode_one, mode_two, mode_three, core_tensor, slab_index):
    n_i, n_j, _ = quantized.shape
    rank = mode_two.shape[1]
    own = core_tensor.shape[0]
    f32, bf16 = jnp.float32, jnp.bfloat16
    vmem = pl.BlockSpec(memory_space=pltpu.VMEM)
    dma = pltpu.SemaphoreType.DMA
    one_t, new_core = pl.pallas_call(
        functools.partial(kernel, n_rows, n_cols),
        out_shape=(
            jax.ShapeDtypeStruct((rank, n_i), f32),
            jax.ShapeDtypeStruct((own, rank, rank), f32),
        ),
        in_specs=[pl.BlockSpec(memory_space=pltpu.SMEM)] + [pl.BlockSpec(memory_space=pl.ANY)] * 6,
        out_specs=(vmem, vmem),
        scratch_shapes=[
            pltpu.VMEM(scales.shape, bf16),
            pltpu.VMEM((rank, n_i), f32),
            pltpu.VMEM((rank, n_j), bf16),
            pltpu.VMEM((rank, mode_three.shape[0]), bf16),
            pltpu.VMEM(core_tensor.shape, f32),
            pltpu.VMEM(quantized.shape, bf16),
            pltpu.VMEM((GROUP * SLAB, GROUP * rank), bf16),
            pltpu.VMEM((STEP, STEP * rank), bf16),
            pltpu.VMEM((n_i * 8, 128), f32),
            pltpu.VMEM((rank * 8, 128), f32),
            pltpu.VMEM((rank * 8, 128), f32),
            pltpu.VMEM((n_cols * rank, rank), f32),
            pltpu.VMEM((n_cols * rank, n_i), f32),
            pltpu.VMEM((n_rows * 8, 128), f32),
            dma((5,)),
            dma((n_i // STEP,)),
            dma((n_rows,)),
            dma((n_rows,)),
            dma((n_cols,)),
            dma((n_cols,)),
            dma((n_cols,)),
            dma((n_cols,)),
            dma((n_rows,)),
            dma((n_rows,)),
        ],
        compiler_params=pltpu.CompilerParams(
            collective_id=0, has_side_effects=True, vmem_limit_bytes=40 * 1024 * 1024
        ),
    )(
        slab_index,
        *(
            pltpu.with_memory_space_constraint(x, pltpu.HBM)
            for x in (quantized, scales, mode_one.T, mode_two.T, mode_three.T, core_tensor)
        ),
    )
    return one_t.T, new_core


def solution(mesh):
    in_specs = (
        P("rows", "cols", None),
        P("rows", "cols"),
        P("rows", None),
        P("cols", None),
        P(),
        P("rows", None, None),
        P(),
    )
    out_specs = (P("rows", None), P("rows", None, None))
    return jax.shard_map(
        functools.partial(local, mesh.shape["rows"], mesh.shape["cols"]),
        mesh=mesh,
        in_specs=in_specs,
        out_specs=out_specs,
        check_vma=False,
    )
```
